32 devices in a mesh: row: 4 (over y, core), col: 8 (over z, x).
Axes of the slice: x: 2, y: 2, z: 4, core: 2. Of those that a mesh axis runs over, the one named last changes fastest.
Arguments:
- inputs: bfloat16 [512, 12288], P('col', 'row'), may hold values from -6 to 6
- grad_out: bfloat16 [512, 12288], P('col', 'row'), may hold values from -6 to 6
- w_in: bfloat16 [12288, 24576], P('row', 'col'), may hold values from -0.0546875 to 0.0546875
- w_out: bfloat16 [24576, 12288], P('col', 'row'), may hold values from -0.0390625 to 0.0390625
Outputs:
- outputs: bfloat16 [512, 12288], P('col', 'row')
- grad_in: bfloat16 [512, 12288], P('col', 'row')
- grad_w_in: bfloat16 [12288, 24576], P('row', 'col')
- grad_w_out: bfloat16 [24576, 12288], P('col', 'row')
The draws below stay inside these ranges and needn't reach their ends.
All inputs are finite; a program needn't handle non-finite values.
Results may differ from the reference program's by a relative error of at most 0.019.
Values may be sent and summed in bfloat16 or wider, within the bound.
A program may use at most 192 MiB of HBM per device.

```python
from functools import partial
import jax
import jax.numpy as jnp
from jax import lax

D = 12288
FF = 24576
TOKENS = 512
N_ROW = 4
N_COL = 8


def shard_levels(rng, dims, pieces, low, largest):
    level, own = 1.0, jax.random.fold_in(rng, 6)
    for axis_at, parts in pieces:
        heights = jnp.exp(jax.random.uniform(jax.random.fold_in(own, axis_at), (parts,), jnp.float32, low / len(pieces), largest / len(pieces)))
        level = level * jnp.repeat(heights, dims[axis_at] // parts).reshape([-1 if axis == axis_at else 1 for axis in range(len(dims))])
    return level


def gaussian(stream_key, dims, scale, limit, split=(), dtype=jnp.bfloat16):
    level = shard_levels(stream_key, dims, split, -0.22, 0.18) if split else 1.0
    result = jax.random.normal(stream_key, dims, jnp.float32) * scale * level
    return jnp.minimum(jnp.maximum(result, -limit), limit).astype(dtype)


def setup_inputs(seed: int = 0) -> dict:
    seeds = jax.random.split(jax.random.key(seed), 5)
    return {
        "inputs": gaussian(seeds[0], (TOKENS, D), 1.0, 6.0, ((0, 8), (1, 4))),
        "grad_out": gaussian(seeds[1], (TOKENS, D), 1.0, 6.0, ((0, 8), (1, 4))),
        "w_in": gaussian(seeds[2], (D, FF), D ** -0.5, 0.0546875, ((0, 4), (1, 8))),
        "w_out": gaussian(seeds[3], (FF, D), FF ** -0.5, 0.0390625, ((0, 8), (1, 4))),
    }


def group_sum(left, right, groups):
    inner = left.shape[1] // groups
    total = jnp.zeros((left.shape[0], right.shape[1]), jnp.float32)
    for group in range(groups):
        lo = group * inner
        term = jnp.dot(left[:, lo:lo + inner], right[lo:lo + inner, :], preferred_element_type=jnp.float32)
        term = lax.optimization_barrier(term.astype(jnp.bfloat16))
        total = total + term.astype(jnp.float32)
    return total

def reference(inputs, grad_out, w_in, w_out):
    gelu_tanh = partial(jax.nn.gelu, approximate=True)
    hidden_pre = group_sum(inputs, w_in, N_ROW)
    act = gelu_tanh(hidden_pre).astype(jnp.bfloat16)
    outputs = group_sum(act, w_out, N_COL).astype(jnp.bfloat16)
    grad_act = group_sum(grad_out, w_out.T, N_ROW)
    grad_pre = jax.vjp(gelu_tanh, hidden_pre)[1](grad_act)[0].astype(jnp.bfloat16)
    grad_w_out = jnp.dot(act.T, grad_out, preferred_element_type=jnp.float32).astype(jnp.bfloat16)
    grad_w_in = jnp.dot(inputs.T, grad_pre, preferred_element_type=jnp.float32).astype(jnp.bfloat16)
    grad_in = group_sum(grad_pre, w_in.T, N_COL).astype(jnp.bfloat16)
    return (outputs, grad_in, grad_w_in, grad_w_out)
```

```python
import functools

import jax
import jax.numpy as jnp
from jax import lax
from jax.experimental import pallas as pl
from jax.experimental.pallas import tpu as pltpu
from jax.sharding import PartitionSpec as P

MESH = pl.DeviceIdType.MESH
NZ = 4
CORES = 2
PARTS = 4
STRIP = 16
VMEM = pl.BlockSpec(memory_space=pltpu.VMEM)
ANY = pl.BlockSpec(memory_space=pl.ANY)


def ring_place(col, nx):
    z, x = col // nx, col % nx
    inner = (x + nx - 1) // nx
    odd = z % 2
    along = (1 - odd) * (x - 1) + odd * (nx - 1 - x)
    return inner * (z * (nx - 1) + along) + (1 - inner) * (NZ * (nx - 1) + NZ - 1 - z)


def ring_col(place, nx):
    back = place // (NZ * (nx - 1))
    z, k = place // (nx - 1), place % (nx - 1)
    odd = z % 2
    x = 1 + (1 - odd) * k + odd * (nx - 2 - k)
    return (1 - back) * (z * nx + x) + back * ((NZ - 1 - (place - NZ * (nx - 1))) * nx)


def greet(axis, others):
    barrier = pltpu.get_barrier_semaphore()
    for other in others:
        pl.semaphore_signal(barrier, inc=1, device_id={axis: other}, device_id_type=MESH)
    pl.semaphore_wait(barrier, len(others))


def rows(start, size):
    return pl.ds(pl.multiple_of(start, STRIP), size)


def col_panels_kernel(n, a_ref, b_ref, a_all, b_all, send_sem, recv_sem, own_sem):
    nx = n // NZ
    place = ring_place(lax.axis_index("col"), nx)
    me = lax.axis_index("col")
    nexts = (ring_col((place + 1) % n, nx), ring_col((place + n - 1) % n, nx))
    size = a_ref.shape[0]
    half = size // 2
    greet("col", nexts)
    streams = [(i, src, dst, d) for i, (src, dst) in enumerate(((a_ref, a_all), (b_ref, b_all))) for d in range(2)]
    own = [pltpu.make_async_copy(src, dst.at[rows(me * size, size)], own_sem.at[i])
           for i, (src, dst) in enumerate(((a_ref, a_all), (b_ref, b_all)))]
    sent = {}
    for step in range(n - 1):
        for i, src, dst, d in streams:
            if step:
                sent[i, d, step - 1].wait_recv()
            origin = ring_col((place + (n - step if d == 0 else step)) % n, nx)
            where = dst.at[rows(origin * size + d * half, half)]
            copy = pltpu.make_async_remote_copy(
                src_ref=where if step else src.at[pl.ds(d * half, half)],
                dst_ref=where,
                send_sem=send_sem.at[i, d, step],
                recv_sem=recv_sem.at[i, d, step],
                device_id={"col": nexts[d]},
                device_id_type=MESH,
            )
            copy.start()
            sent[i, d, step] = copy
        if step == 0:
            for copy in own:
                copy.start()
    for i, _, _, d in streams:
        sent[i, d, n - 2].wait_recv()
    for copy in sent.values():
        copy.wait_send()
    for copy in own:
        copy.wait()


def col_panels(n, a, b):
    full = jax.ShapeDtypeStruct((a.shape[0] * n, a.shape[1]), a.dtype)
    return pl.pallas_call(
        functools.partial(col_panels_kernel, n),
        out_shape=(full, full),
        in_specs=[VMEM, VMEM],
        out_specs=(VMEM, VMEM),
        scratch_shapes=[
            pltpu.SemaphoreType.DMA((2, 2, n - 1)),
            pltpu.SemaphoreType.DMA((2, 2, n - 1)),
            pltpu.SemaphoreType.DMA((2,)),
        ],
        compiler_params=pltpu.CompilerParams(collective_id=0, has_side_effects=True),
    )(a, b)


def hidden_kernel(n, h_ref, g_ref, act_ref, pre_ref, near, far, stage, near_sems, far_sems, y_sems, core_sems):
    ny = n // CORES
    me = lax.axis_index("row")
    y, core = me // CORES, me % CORES
    mate = y * CORES + 1 - core
    up = ((y + 1) % ny) * CORES + core
    down = ((y + ny - 1) % ny) * CORES + core
    greet("row", (mate, up) if ny == 2 else (mate, up, down))
    tokens, wide = h_ref.shape
    size = tokens // n
    width = wide // PARTS
    parts = ((0, h_ref), (1, g_ref))
    columns = [pl.ds(f * width, width) for f in range(PARTS)]

    def send(src, dst, sems, where, device):
        copy = pltpu.make_async_remote_copy(
            src_ref=src, dst_ref=dst, send_sem=sems.at[(0, *where)], recv_sem=sems.at[(1, *where)],
            device_id={"row": device}, device_id_type=MESH)
        copy.start()
        return copy

    copies, near_copies, far_copies = [], {}, {}
    for k in range(ny):
        block = (y + ny - 1 - k) % ny
        for f in range(PARTS):
            for i, ref in parts:
                near_copies[i, k, f] = send(
                    ref.at[rows(((1 - core) * ny + block) * size, size), columns[f]],
                    near.at[i, k, :, columns[f]], near_sems, (i, k, f), mate)

    for k in range(ny - 1):
        base = (core * ny + (y + ny - 1 - k) % ny) * size
        for f in range(PARTS):
            for i, ref in parts:
                near_copies[i, k, f].wait_recv()
                if k:
                    far_copies[i, k - 1, f].wait_recv()

                @pl.loop(0, size // STRIP)
                def _(r):
                    strip = rows(r * STRIP, STRIP)
                    total = ref[rows(base + r * STRIP, STRIP), columns[f]].astype(jnp.float32)
                    total += near[i, k, strip, columns[f]].astype(jnp.float32)
                    if k:
                        total += far[i, k - 1, strip, columns[f]].astype(jnp.float32)
                    stage[i, k, strip, columns[f]] = total.astype(jnp.bfloat16)

                far_copies[i, k, f] = send(
                    stage.at[i, k, :, columns[f]], far.at[i, k, :, columns[f]], far_sems, (i, k, f), up)

    mine = (core * ny + y) * size
    scale = 0.7978845608028654
    ring, swaps = {}, []
    outs = ((0, act_ref), (1, pre_ref))
    for f in range(PARTS):
        for i, _ in parts:
            near_copies[i, ny - 1, f].wait_recv()
            far_copies[i, ny - 2, f].wait_recv()

        @pl.loop(0, size // STRIP)
        def _(r):
            strip = rows(r * STRIP, STRIP)
            full = rows(mine + r * STRIP, STRIP)

            def total(i, ref):
                return (ref[full, columns[f]].astype(jnp.float32)
                        + near[i, ny - 1, strip, columns[f]].astype(jnp.float32)
                        + far[i, ny - 2, strip, columns[f]].astype(jnp.float32))

            v, g = total(0, h_ref), total(1, g_ref)
            square = v * v
            t = jnp.tanh(scale * v * (1.0 + 0.044715 * square))
            act_ref[full, columns[f]] = (0.5 * v * (1.0 + t)).astype(jnp.bfloat16)
            slope = 0.5 * (1.0 + t) + (0.5 * scale) * v * (1.0 - t * t) * (1.0 + 0.134145 * square)
            pre_ref[full, columns[f]] = (slope * g).astype(jnp.bfloat16)

        for i, out in outs:
            where = out.at[rows(mine, size), columns[f]]
            ring[i, 0, f] = send(where, where, y_sems, (i, 0, f), up)
            swaps.append(send(where, where, core_sems, (i, 0, f), mate))
    for k in range(1, ny):
        for f in range(PARTS):
            for i, out in outs:
                ring[i, k - 1, f].wait_recv()
                where = out.at[rows((core * ny + (y + ny - k) % ny) * size, size), columns[f]]
                if k < ny - 1:
                    ring[i, k, f] = send(where, where, y_sems, (i, k, f), up)
                swaps.append(send(where, where, core_sems, (i, k, f), mate))
    for copy in swaps:
        copy.wait()
    for group in (near_copies, far_copies, ring):
        for copy in group.values():
            copy.wait_send()


def hidden(n, h_part, g_part):
    tokens, wide = h_part.shape
    ny, size = n // CORES, tokens // n
    full = jax.ShapeDtypeStruct((tokens, wide), jnp.bfloat16)
    return pl.pallas_call(
        functools.partial(hidden_kernel, n),
        out_shape=(full, full),
        in_specs=[VMEM, VMEM],
        out_specs=(VMEM, VMEM),
        scratch_shapes=[
            pltpu.VMEM((2, ny, size, wide), jnp.bfloat16),
            pltpu.VMEM((2, ny - 1, size, wide), jnp.bfloat16),
            pltpu.VMEM((2, ny - 1, size, wide), jnp.bfloat16),
            pltpu.SemaphoreType.DMA((2, 2, ny, PARTS)),
            pltpu.SemaphoreType.DMA((2, 2, ny - 1, PARTS)),
            pltpu.SemaphoreType.DMA((2, 2, ny - 1, PARTS)),
            pltpu.SemaphoreType.DMA((2, 2, ny, PARTS)),
        ],
        compiler_params=pltpu.CompilerParams(collective_id=1, has_side_effects=True),
    )(h_part, g_part)


def col_sums_kernel(n, a_ref, b_ref, a_out, b_out, held, send_sem, recv_sem):
    nx = n // NZ
    place = ring_place(lax.axis_index("col"), nx)
    me = lax.axis_index("col")
    nexts = (ring_col((place + 1) % n, nx), ring_col((place + n - 1) % n, nx))
    size, wide = a_out.shape
    half = wide // 2
    greet("col", nexts)
    streams = [(i, ref, out, d) for d in range(2) for i, (ref, out) in enumerate(((a_ref, a_out), (b_ref, b_out)))]
    sent = {}
    for step in range(n):
        for i, ref, out, d in streams:
            block = ring_col((place + (2 * n - 1 - step if d == 0 else 1 + step)) % n, nx) if step < n - 1 else me
            columns = pl.ds(d * half, half)
            if step:
                sent[i, d, step - 1].wait_recv()

                @pl.loop(0, size // STRIP)
                def _(r):
                    strip = rows(r * STRIP, STRIP)
                    total = held[i, d, step - 1, strip, :].astype(jnp.float32)
                    total += ref[rows(block * size + r * STRIP, STRIP), columns].astype(jnp.float32)
                    if step < n - 1:
                        held[i, d, step - 1, strip, :] = total.astype(jnp.bfloat16)
                    else:
                        out[strip, columns] = total.astype(jnp.bfloat16)

            if step < n - 1:
                copy = pltpu.make_async_remote_copy(
                    src_ref=held.at[i, d, step - 1] if step else ref.at[rows(block * size, size), columns],
                    dst_ref=held.at[i, d, step],
                    send_sem=send_sem.at[i, d, step],
                    recv_sem=recv_sem.at[i, d, step],
                    device_id={"col": nexts[d]},
                    device_id_type=MESH,
                )
                copy.start()
                sent[i, d, step] = copy
    for copy in sent.values():
        copy.wait_send()


def col_sums(n, a, b):
    size, wide = a.shape[0] // n, a.shape[1]
    part = jax.ShapeDtypeStruct((size, wide), jnp.bfloat16)
    return pl.pallas_call(
        functools.partial(col_sums_kernel, n),
        out_shape=(part, part),
        in_specs=[VMEM, VMEM],
        out_specs=(VMEM, VMEM),
        scratch_shapes=[
            pltpu.VMEM((2, 2, n - 1, size, wide // 2), jnp.bfloat16),
            pltpu.SemaphoreType.DMA((2, 2, n - 1)),
            pltpu.SemaphoreType.DMA((2, 2, n - 1)),
        ],
        compiler_params=pltpu.CompilerParams(collective_id=2, has_side_effects=True),
    )(a, b)


def contract(left, right, dims):
    return lax.dot_general(
        left, right, ((dims[0], dims[1]), ((), ())), preferred_element_type=jnp.float32
    ).astype(jnp.bfloat16)


def solution(mesh):
    n_row, n_col = mesh.shape["row"], mesh.shape["col"]

    def local(inputs, grad_out, w_in, w_out):
        input_all, cotan_all = col_panels(n_col, inputs, grad_out)
        act_all, grad_pre_all = hidden(
            n_row,
            contract(input_all, w_in, ((1,), (0,))),
            contract(cotan_all, w_out, ((1,), (1,))),
        )
        outputs, grad_in = col_sums(
            n_col,
            contract(act_all, w_out, ((1,), (0,))),
            contract(grad_pre_all, w_in, ((1,), (1,))),
        )
        grad_w_out = contract(act_all, cotan_all, ((0,), (0,)))
        grad_w_in = contract(input_all, grad_pre_all, ((0,), (0,)))
        return (outputs, grad_in, grad_w_in, grad_w_out)

    placed = (P("col", "row"), P("col", "row"), P("row", "col"), P("col", "row"))
    return jax.shard_map(local, mesh=mesh, in_specs=placed, out_specs=placed, check_vma=False)
```

```python
import functools

import jax
import jax.numpy as jnp
from jax import lax
from jax.experimental import pallas as pl
from jax.experimental.pallas import tpu as pltpu
from jax.sharding import PartitionSpec as P

MESH = pl.DeviceIdType.MESH
NZ = 4
CORES = 2
PARTS = 4
SUBS = 2
LANES = 256
STRIP = 16
VMEM = pl.BlockSpec(memory_space=pltpu.VMEM)
ANY = pl.BlockSpec(memory_space=pl.ANY)


def ring_place(col, nx):
    z, x = col // nx, col % nx
    inner = (x + nx - 1) // nx
    odd = z % 2
    along = (1 - odd) * (x - 1) + odd * (nx - 1 - x)
    return inner * (z * (nx - 1) + along) + (1 - inner) * (NZ * (nx - 1) + NZ - 1 - z)


def ring_col(place, nx):
    back = place // (NZ * (nx - 1))
    z, k = place // (nx - 1), place % (nx - 1)
    odd = z % 2
    x = 1 + (1 - odd) * k + odd * (nx - 2 - k)
    return (1 - back) * (z * nx + x) + back * ((NZ - 1 - (place - NZ * (nx - 1))) * nx)


def greet(others):
    barrier = pltpu.get_barrier_semaphore()
    for other in others:
        pl.semaphore_signal(barrier, inc=1, device_id=other, device_id_type=MESH)
    pl.semaphore_wait(barrier, len(others))


def rows(start, size):
    return pl.ds(pl.multiple_of(start, STRIP), size)


def layer_kernel(
    n_row, n_col, x_ref, c_ref, w_in, w_out, x_all, c_all, act_ref, pre_ref, out_ref, gin_ref,
    h_ref, g_ref, o_ref, i_ref, near, far, stage, slope_ref, held, by_col, by_row,
    own_sem, w_sem, ag_sems, near_sems, far_sems, y_sems, core_sems, rs_sems,
):
    nx, ny = n_col // NZ, n_row // CORES
    here = lax.axis_index("col")
    place = ring_place(here, nx)
    nexts = [{"col": ring_col((place + 1) % n_col, nx)}, {"col": ring_col((place + n_col - 1) % n_col, nx)}]
    me = lax.axis_index("row")
    y, core = me // CORES, me % CORES
    mate = {"row": y * CORES + 1 - core}
    up = {"row": ((y + 1) % ny) * CORES + core}
    down = {"row": ((y + ny - 1) % ny) * CORES + core}
    greet(nexts + [mate, up] + ([] if ny == 2 else [down]))
    size, wide = x_ref.shape
    tokens = x_all.shape[0]
    fine = tokens // n_row
    width = wide // PARTS
    lanes = LANES if width % LANES == 0 else LANES // 2
    columns = [pl.ds(f * width, width) for f in range(PARTS)]
    loose = []

    def send(src, dst, sems, where, device):
        copy = pltpu.make_async_remote_copy(
            src_ref=src, dst_ref=dst, send_sem=sems.at[(0, *where)], recv_sem=sems.at[(1, *where)],
            device_id=device, device_id_type=MESH)
        copy.start()
        loose.append(copy)
        return copy

    def gather(i, src, dst):
        piece = size // (2 * SUBS)
        flows = [(d, s) for s in range(SUBS) for d in range(2)]
        last = {}
        for step in range(n_col - 1):
            for d, s in flows:
                if step:
                    last[d, s].wait_recv()
                at = (d * SUBS + s) * piece
                origin = ring_col((place + (n_col - step if d == 0 else step)) % n_col, nx)
                where = dst.at[rows(origin * size + at, piece)]
                last[d, s] = send(where if step else src.at[pl.ds(at, piece)], where, ag_sems, (i, d, s, step), nexts[d])
            if step == 0:
                own = pltpu.make_async_copy(src, dst.at[rows(here * size, size)], own_sem.at[i])
                own.start()
            yield
        for copy in last.values():
            copy.wait_recv()
        own.wait()
        yield

    tiles = []
    for kind, weight in ((0, w_in), (1, w_out), (0, w_out), (1, w_in)):
        for f in range(PARTS):
            tiles.append((kind, f % 2, weight.at[:, columns[f]] if kind == 0 else weight.at[columns[f], :]))

    def fetch(j):
        kind, slot, src = tiles[j]
        return pltpu.make_async_copy(src, (by_row if kind else by_col).at[slot], w_sem.at[kind, slot])

    def product(j, left, dst):
        kind, slot, _ = tiles[j]
        fetch(j).wait()
        if j + 1 < len(tiles):
            fetch(j + 1).start()
        f = j % PARTS

        @pl.loop(0, width // lanes)
        def _(t):
            at = pl.ds(pl.multiple_of(t * lanes, lanes), lanes)
            right = by_row[slot, at, :] if kind else by_col[slot, :, at]
            total = lax.dot_general(left[...], right, (((1,), (kind,)), ((), ())),
                                    preferred_element_type=jnp.float32)
            dst[:, pl.ds(pl.multiple_of(f * width + t * lanes, lanes), lanes)] = total.astype(jnp.bfloat16)

    scale = 0.7978845608028654
    swaps = {0: [], 1: []}

    def exchange(i, f, ref, out):
        cols = columns[f]
        got_near, got_far, ring = [], [], []
        for k in range(ny):
            block = (y + ny - 1 - k) % ny
            got_near.append(send(ref.at[rows(((1 - core) * ny + block) * fine, fine), cols],
                                 near.at[i, k, :, cols], near_sems, (i, k, f), mate))
        yield
        for k in range(ny - 1):
            base = (core * ny + (y + ny - 1 - k) % ny) * fine
            got_near[k].wait_recv()
            if k:
                got_far[k - 1].wait_recv()

            @pl.loop(0, fine // STRIP)
            def _(r):
                strip = rows(r * STRIP, STRIP)
                total = ref[rows(base + r * STRIP, STRIP), cols].astype(jnp.float32)
                total += near[i, k, strip, cols].astype(jnp.float32)
                if k:
                    total += far[i, k - 1, strip, cols].astype(jnp.float32)
                stage[i, k, strip, cols] = total.astype(jnp.bfloat16)

            got_far.append(send(stage.at[i, k, :, cols], far.at[i, k, :, cols], far_sems, (i, k, f), up))
            yield
        got_near[ny - 1].wait_recv()
        got_far[ny - 2].wait_recv()
        mine = (core * ny + y) * fine

        @pl.loop(0, fine // STRIP)
        def _(r):
            strip = rows(r * STRIP, STRIP)
            full = rows(mine + r * STRIP, STRIP)
            v = (ref[full, cols].astype(jnp.float32) + near[i, ny - 1, strip, cols].astype(jnp.float32)
                 + far[i, ny - 2, strip, cols].astype(jnp.float32))
            if i == 0:
                square = v * v
                t = jnp.tanh(scale * v * (1.0 + 0.044715 * square))
                out[full, cols] = (0.5 * v * (1.0 + t)).astype(jnp.bfloat16)
                slope_ref[strip, cols] = (
                    0.5 * (1.0 + t) + (0.5 * scale) * v * (1.0 - t * t) * (1.0 + 0.134145 * square))
            else:
                out[full, cols] = (slope_ref[strip, cols] * v).astype(jnp.bfloat16)

        where = out.at[rows(mine, fine), cols]
        ring.append(send(where, where, y_sems, (i, 0, f), up))
        swaps[i].append(send(where, where, core_sems, (i, 0, f), mate))
        yield
        for k in range(1, ny):
            ring[k - 1].wait_recv()
            where = out.at[rows((core * ny + (y + ny - k) % ny) * fine, fine), cols]
            if k < ny - 1:
                ring.append(send(where, where, y_sems, (i, k, f), up))
            swaps[i].append(send(where, where, core_sems, (i, k, f), mate))
            yield

    def reduce(i, f, ref, out):
        d, cols = f % 2, columns[f]
        copy = None
        for step in range(n_col):
            final = step == n_col - 1
            block = here if final else ring_col((place + (2 * n_col - 1 - step if d == 0 else 1 + step)) % n_col, nx)
            if step:
                copy.wait_recv()

                @pl.loop(0, size // STRIP)
                def _(r):
                    strip = rows(r * STRIP, STRIP)
                    total = held[i, f, step - 1, strip, :].astype(jnp.float32)
                    total += ref[rows(block * size + r * STRIP, STRIP), cols].astype(jnp.float32)
                    if final:
                        out[strip, cols] = total.astype(jnp.bfloat16)
                    else:
                        held[i, f, step - 1, strip, :] = total.astype(jnp.bfloat16)

            if not final:
                copy = send(held.at[i, f, step - 1] if step else ref.at[rows(block * size, size), cols],
                            held.at[i, f, step], rs_sems, (i, f, step), nexts[d])
            yield

    def go(*flows):
        for flow in flows:
            next(flow, None)

    def drain(flows):
        for _ in range(n_col + 2):
            go(*flows)

    fetch(0).start()
    inward = gather(0, x_ref, x_all)
    for _ in range(n_col):
        go(inward)
    other = gather(1, c_ref, c_all)
    acts = [exchange(0, f, h_ref, act_ref) for f in range(PARTS)]
    pres = [exchange(1, f, g_ref, pre_ref) for f in range(PARTS)]
    outs = [reduce(0, f, o_ref, out_ref) for f in range(PARTS)]
    gins = [reduce(1, f, i_ref, gin_ref) for f in range(PARTS)]
    go(other)
    for f in range(PARTS):
        product(f, x_all, h_ref)
        go(acts[f], *acts[f - 1:f], other)
    go(acts[-1])
    for _ in range(ny - 2):
        go(*acts)
    for f in range(PARTS):
        go(acts[f], other)
    for _ in range(n_col):
        go(other)
    for f in range(PARTS):
        product(PARTS + f, c_all, g_ref)
        go(pres[f], *pres[f - 1:f], acts[f])
    go(pres[-1])
    for _ in range(ny - 2):
        go(*acts)
        go(*pres)
    for copy in swaps[0]:
        copy.wait_recv()
    for f in range(PARTS):
        product(2 * PARTS + f, act_ref, o_ref)
        go(outs[f], pres[f], *outs[:f])
    for _ in range(ny - 1):
        for f in range(PARTS):
            go(pres[f], outs[f])
    for copy in swaps[1]:
        copy.wait_recv()
    for f in range(PARTS):
        product(3 * PARTS + f, pre_ref, i_ref)
        go(gins[f], *outs, *gins[:f])
    drain(outs + gins)
    for copy in loose:
        copy.wait_send()


def layer(n_row, n_col, x, c, w_in, w_out):
    size, wide = x.shape
    tokens = size * n_col
    ny, fine = n_row // CORES, tokens // n_row
    width = wide // PARTS
    full = jax.ShapeDtypeStruct((tokens, wide), jnp.bfloat16)
    part = jax.ShapeDtypeStruct((size, wide), jnp.bfloat16)
    dma = pltpu.SemaphoreType.DMA
    half = functools.partial(pltpu.VMEM, dtype=jnp.bfloat16)
    return pl.pallas_call(
        functools.partial(layer_kernel, n_row, n_col),
        out_shape=(full, full, full, full, part, part),
        in_specs=[VMEM, VMEM, ANY, ANY],
        out_specs=(VMEM,) * 6,
        scratch_shapes=[
            half((tokens, wide)), half((tokens, wide)), half((tokens, wide)), half((tokens, wide)),
            half((2, ny, fine, wide)),
            half((2, ny - 1, fine, wide)),
            half((2, ny - 1, fine, wide)),
            pltpu.VMEM((fine, wide), jnp.float32),
            half((2, PARTS, n_col - 1, size, width)),
            half((2, wide, width)),
            half((2, width, wide)),
            dma((2,)),
            dma((2, 2)),
            dma((2, 2, 2, SUBS, n_col - 1)),
            dma((2, 2, ny, PARTS)),
            dma((2, 2, ny - 1, PARTS)),
            dma((2, 2, ny - 1, PARTS)),
            dma((2, 2, ny, PARTS)),
            dma((2, 2, PARTS, n_col - 1)),
        ],
        compiler_params=pltpu.CompilerParams(
            collective_id=0, has_side_effects=True, vmem_limit_bytes=67043328),
    )(x, c, w_in, w_out)


def contract(left, right, dims):
    return lax.dot_general(
        left, right, ((dims[0], dims[1]), ((), ())), preferred_element_type=jnp.float32
    ).astype(jnp.bfloat16)


def solution(mesh):
    n_row, n_col = mesh.shape["row"], mesh.shape["col"]

    def local(inputs, grad_out, w_in, w_out):
        input_all, cotan_all, act_all, grad_pre_all, outputs, grad_in = layer(
            n_row, n_col, inputs, grad_out, w_in, w_out)
        grad_w_out = contract(act_all, cotan_all, ((0,), (0,)))
        grad_w_in = contract(input_all, grad_pre_all, ((0,), (0,)))
        return (outputs, grad_in, grad_w_in, grad_w_out)

    placed = (P("col", "row"), P("col", "row"), P("row", "col"), P("col", "row"))
    return jax.shard_map(local, mesh=mesh, in_specs=placed, out_specs=placed, check_vma=False)
```
